32 devices in a mesh: ctx: 8 (over z, y), fsdp: 4 (over x, core).
Axes of the slice: x: 2, y: 2, z: 4, core: 2. Of those that a mesh axis runs over, the one named last changes fastest.
Arguments:
- hidden_in: float32 [4, 2048, 1024], P('fsdp', 'ctx'), may hold values from -6 to 6
- positions: int32 [4, 2048], P('fsdp', 'ctx'), may hold values from 0 to 1023, as said below
- mixer_gain: bfloat16 [1024], P('fsdp'), may hold values from 0.5 to 1.5
- attention_in: bfloat16 [1024, 768], P('fsdp'), may hold values from -16 to 16
- attention_out: bfloat16 [512, 1024], P('fsdp'), may hold values from -2 to 2
- mamba_in: bfloat16 [1024, 3352], P('fsdp'), may hold values from -0.1875 to 0.1875
- filter_taps: bfloat16 [4, 1792], P(None, 'fsdp'), may hold values from -3 to 3
- step_bias: bfloat16 [24], P('fsdp'), may hold values from -3 to -1
- decay_log: bfloat16 [24], P('fsdp')
- skip_gain: bfloat16 [24], P('fsdp'), may hold values from 0.5 to 2
- gated_gain: bfloat16 [1536], P('fsdp'), may hold values from 0.5 to 1.5
- mamba_out: bfloat16 [1536, 1024], P('fsdp'), may hold values from -0.15625 to 0.15625
- feed_gain: bfloat16 [1024], P('fsdp'), may hold values from 0.5 to 1.5
- gate_weight: bfloat16 [1024, 2048], P(None, 'fsdp'), may hold values from -0.1875 to 0.1875
- up_weight: bfloat16 [1024, 2048], P(None, 'fsdp'), may hold values from -0.1875 to 0.1875
- down_weight: bfloat16 [2048, 1024], P('fsdp'), may hold values from -0.125 to 0.125
- cotangent: float32 [4, 2048, 1024], P('fsdp', 'ctx'), may hold values from -6 to 6
Outputs:
- hidden_out: float32 [4, 2048, 1024], P('fsdp', 'ctx')
- input_gradient: float32 [4, 2048, 1024], P('fsdp', 'ctx')
- mixer_gain_gradient: float32 [1024], P('fsdp')
- attention_in_gradient: float32 [1024, 768], P('fsdp')
- attention_out_gradient: float32 [512, 1024], P('fsdp')
- mamba_in_gradient: float32 [1024, 3352], P('fsdp')
- filter_taps_gradient: float32 [4, 1792], P(None, 'fsdp')
- step_bias_gradient: float32 [24], P('fsdp')
- decay_log_gradient: float32 [24], P('fsdp')
- skip_gain_gradient: float32 [24], P('fsdp')
- gated_gain_gradient: float32 [1536], P('fsdp')
- mamba_out_gradient: float32 [1536, 1024], P('fsdp')
- feed_gain_gradient: float32 [1024], P('fsdp')
- gate_weight_gradient: float32 [1024, 2048], P(None, 'fsdp')
- up_weight_gradient: float32 [1024, 2048], P(None, 'fsdp')
- down_weight_gradient: float32 [2048, 1024], P('fsdp')
The draws below stay inside these ranges and needn't reach their ends.
Inputs may be any that keep to these rules, and one draw needn't show every extreme that they name: `positions`: each row holds documents laid end to end: an entry is the token's offset from the first token of its document, 0 at a document's first token and rising by one within it. In each row one document spans exactly 1024 tokens and no document spans more.
All inputs are finite; a program needn't handle non-finite values.
Results may differ from the reference program's by a relative error of at most 0.028.
Values may be sent and summed in bfloat16 or wider, within the bound.
No kernel may reach another device: no remote copies, remote signals or barrier semaphores. Data moves between devices by JAX's collectives and lax.ppermute only.
A program may use at most 256 MiB of HBM per device.

```python
import math
import jax
import jax.numpy as jnp
from jax import lax

D = 1024
QHEADS = 8
KVHEADS = 2
HEAD = 64
MHEADS = 24
MHEAD = 64
STATE = 128
CONV = 4
FF = 2048
L_DEV = 256
DIN = 1536
XBC = 1792
QDIM = 512
KVDIM = 128
PROJ = 768
MPROJ = 3352
SEQ = 2048
NSEQ = 4


def draw_positions(key, part):

    def single(seq_key):
        start_key, cut_key = jax.random.split(seq_key)
        half = SEQ // 2
        begin = jax.random.randint(start_key, (), 0, SEQ - half + 1)
        index = jnp.arange(SEQ, dtype=jnp.int32)
        cuts = jax.random.randint(cut_key, (SEQ,), 0, SEQ) < 6
        inside = (index > begin) & (index < begin + half)
        boundary = (index == 0) | (index == begin) | (index == begin + half) | cuts & jnp.logical_not(inside)
        latest = lax.cummax(jnp.where(boundary, index, 0), axis=0)
        return (index - latest).astype(jnp.int32)
    return jax.vmap(single)(jax.random.split(key, NSEQ))


def draw_attention_in(key, part):
    base_key = jax.random.fold_in(key, 0)
    base = jnp.clip(jax.random.normal(base_key, (D, PROJ), jnp.float32), -4.0, 4.0) * D ** (-0.5)
    return base.astype(jnp.bfloat16)


def draw_decay_log(key, part):
    pick_key, jitter_key = jax.random.split(key)
    share = 0.5
    slow = jax.random.uniform(pick_key, (MHEADS,), jnp.float32) < share
    rate = jnp.where(slow, 7.5 / SEQ, 0.125)
    return (jnp.log(rate) + jax.random.uniform(jitter_key, (MHEADS,), jnp.float32, -0.4, 0.4)).astype(jnp.bfloat16)


def level_of(key, extent, cuts, smallest, high):
    level, own = 1.0, jax.random.fold_in(key, 6)
    for dim, parts in cuts:
        heights = jnp.exp(jax.random.uniform(jax.random.fold_in(own, dim), (parts,), jnp.float32, smallest / len(cuts), high / len(cuts)))
        level = level * jnp.repeat(heights, extent[dim] // parts).reshape([-1 if axis == dim else 1 for axis in range(len(extent))])
    return level


def centred(own_key, dims, spread, bound, cuts=(), kind=jnp.bfloat16):
    values = jax.random.normal(own_key, dims, jnp.float32) * spread
    if len(cuts) > 0:
        values = level_of(own_key, dims, cuts, -0.22, 0.18) * values
    return jnp.clip(values, min=-bound, max=bound).astype(kind)


def setup_inputs(seed: int = 0) -> dict:
    streams_of = jax.random.split(jax.random.key(seed), 18)
    return {
        "hidden_in": centred(streams_of[0], (NSEQ, SEQ, D), 1.0, 6.0, ((0, 4), (1, 8)), jnp.float32),
        "positions": draw_positions(jax.random.fold_in(streams_of[17], 71), 0),
        "mixer_gain": jnp.clip(1.0 + 0.1 * jax.random.normal(streams_of[2], (D,), jnp.float32), 0.5, 1.5).astype(jnp.bfloat16),
        "attention_in": draw_attention_in(jax.random.fold_in(streams_of[17], 71), 0),
        "attention_out": centred(streams_of[4], (QDIM, D), (HEAD // 8) ** -0.5, 2.0, ((0, 4),)),
        "mamba_in": centred(streams_of[5], (D, MPROJ), D ** -0.5, 0.1875, ((0, 4),)),
        "filter_taps": centred(streams_of[6], (CONV, XBC), CONV ** -0.5, 3.0, ((1, 4),)),
        "step_bias": jnp.clip(-3.0 + 2.0 * jax.random.uniform(streams_of[7], (MHEADS,), jnp.float32) ** level_of(streams_of[7], (MHEADS,), ((0, 4),), -0.2, 0.2), -3.0, -1.0).astype(jnp.bfloat16),
        "decay_log": draw_decay_log(jax.random.fold_in(streams_of[17], 71), 0),
        "skip_gain": jnp.clip(jnp.exp(math.log(2.0) - 1.3862944 * jax.random.uniform(streams_of[9], (MHEADS,), jnp.float32) ** level_of(streams_of[9], (MHEADS,), ((0, 4),), -0.2, 0.2)), 0.5, 2.0).astype(jnp.bfloat16),
        "gated_gain": jnp.clip(1.0 + 0.1 * jax.random.normal(streams_of[10], (DIN,), jnp.float32), 0.5, 1.5).astype(jnp.bfloat16),
        "mamba_out": centred(streams_of[11], (DIN, D), DIN ** -0.5, 0.15625, ((0, 4),)),
        "feed_gain": jnp.clip(1.0 + 0.1 * jax.random.normal(streams_of[12], (D,), jnp.float32), 0.5, 1.5).astype(jnp.bfloat16),
        "gate_weight": centred(streams_of[13], (D, FF), D ** -0.5, 0.1875, ((1, 4),)),
        "up_weight": centred(streams_of[14], (D, FF), D ** -0.5, 0.1875, ((1, 4),)),
        "down_weight": centred(streams_of[15], (FF, D), FF ** -0.5, 0.125, ((0, 4),)),
        "cotangent": centred(streams_of[16], (NSEQ, SEQ, D), 1.0, 6.0, ((0, 4), (1, 8)), jnp.float32),
    }


EPS = 1e-05
NEGATIVE = -1e+30
ROPE_BASE = 10000.0
HIGH = lax.Precision.HIGHEST

def matmul(left, right):
    return jnp.dot(left, right, preferred_element_type=jnp.float32)

def rms_forward(values, gain):
    inverse = lax.rsqrt(lax.optimization_barrier(jnp.mean(values * values, axis=-1, keepdims=True)) + EPS)
    return (values * inverse * gain, inverse)

def rms_backward(values, inverse, gain, upstream):
    scaled = gain * upstream
    inner = lax.optimization_barrier(jnp.mean(scaled * values, axis=-1, keepdims=True))
    back = inverse * scaled - values * inverse ** 3 * inner
    return (back, lax.optimization_barrier(jnp.sum(upstream * values * inverse, axis=0)))

def rotary_tables(token_pos, half):
    exponent = jnp.arange(half, dtype=jnp.float32) * (2.0 / (2 * half))
    frequency = jnp.exp(-math.log(ROPE_BASE) * exponent)
    angle = token_pos.astype(jnp.float32)[:, None] * frequency[None, :]
    return (jnp.cos(angle), jnp.sin(angle))

def rotate(tensor, cosine, sine):
    half = tensor.shape[-1] // 2
    first = tensor[..., :half]
    second = tensor[..., half:]
    cos_part = cosine[:, None, :]
    sin_part = sine[:, None, :]
    return jnp.concatenate([first * cos_part - second * sin_part, second * cos_part + first * sin_part], axis=-1)

def rotate_back(tensor, cosine, sine):
    half = tensor.shape[-1] // 2
    first = tensor[..., :half]
    second = tensor[..., half:]
    cos_part = cosine[:, None, :]
    sin_part = sine[:, None, :]
    return jnp.concatenate([first * cos_part + second * sin_part, second * cos_part - first * sin_part], axis=-1)

def group_rows(tensor, groups):
    count, heads, width = tensor.shape
    members = heads // groups
    return tensor.reshape(count, groups, members, width).transpose(1, 2, 0, 3).reshape(groups, members * count, width)

def ungroup_rows(tensor, count):
    groups, rows, width = tensor.shape
    members = rows // count
    return tensor.reshape(groups, members, count, width).transpose(2, 0, 1, 3).reshape(count, groups * members, width)

def mixer_inputs(window, step_raw, taps, step_bias, decay_log):
    span = step_raw.shape[0]
    convolved = taps[0] * window[0:span]
    for tap in range(1, taps.shape[0]):
        convolved = convolved + taps[tap] * window[tap:tap + span]
    activated = jax.nn.silu(convolved)
    inner = activated[:, :DIN].reshape(span, MHEADS, MHEAD)
    basis = activated[:, DIN:DIN + STATE]
    reader = activated[:, DIN + STATE:]
    step = jax.nn.softplus(step_raw + step_bias)
    logdecay = -step * jnp.exp(decay_log)
    return (inner, basis, reader, step, logdecay)

def block_states(inner, basis, step, logdecay):
    cumulative = jnp.cumsum(logdecay, axis=0)
    weight = jnp.exp(cumulative[-1][None, :] - cumulative) * step
    state = jnp.einsum('thp,tn->hpn', inner * weight[:, :, None], basis, precision=HIGH)
    return (state, jnp.exp(cumulative[-1]))

def block_outputs(inner, basis, reader, step, logdecay, incoming, gate_z, skip):
    span = step.shape[0]
    cumulative = jnp.cumsum(logdecay, axis=0)
    intersection = jnp.dot(reader, basis.T, precision=HIGH)
    order = jnp.arange(span, dtype=jnp.int32)
    causal = (order[:, None] >= order[None, :])[:, :, None]
    gap = cumulative[:, None, :] - cumulative[None, :, :]
    decay = jnp.where(causal, jnp.exp(jnp.where(causal, gap, 0.0)), 0.0)
    mixing = intersection[:, :, None] * decay * step[None, :, :]
    within = jnp.einsum('tsh,shp->thp', mixing, inner, precision=HIGH)
    carried = jnp.exp(cumulative)[:, :, None] * jnp.einsum('tn,hpn->thp', reader, incoming, precision=HIGH)
    output = within + carried + skip[None, :, None] * inner
    return output.reshape(span, -1) * jax.nn.silu(gate_z)

def feed_forward(rows, gate_w, up_w):
    gate = matmul(rows, gate_w)
    up = matmul(rows, up_w)
    activated = (jax.nn.silu(gate) * up).astype(jnp.bfloat16)
    return (gate, up, activated)

def feed_backward(rows, gate, up, activated, upstream_b, gate_w, up_w, down_w):
    down_grad = matmul(activated.T, upstream_b)
    act_grad = matmul(upstream_b, down_w.T)
    sigma = jax.nn.sigmoid(gate)
    gate_part = (act_grad * up * sigma * (1.0 + gate * (1.0 - sigma))).astype(jnp.bfloat16)
    up_part = (act_grad * gate * sigma).astype(jnp.bfloat16)
    gate_grad = matmul(rows.T, gate_part)
    up_grad = matmul(rows.T, up_part)
    back = matmul(gate_part, gate_w.T) + matmul(up_part, up_w.T)
    return (gate_grad, up_grad, down_grad, back)

def mamba_sequence(conv_f, step_raw, gate_z, taps, step_bias, decay_log, skip):
    total_rows, width = conv_f.shape
    span = L_DEV
    count = total_rows // span
    padded = jnp.concatenate([jnp.zeros((CONV - 1, width), jnp.float32), conv_f], axis=0)

    def prepare(index):
        start = index * span
        window = lax.dynamic_slice_in_dim(padded, start, span + CONV - 1, 0)
        raw = lax.dynamic_slice_in_dim(step_raw, start, span, 0)
        return mixer_inputs(window, raw, taps, step_bias, decay_log)
    inner, basis, reader, step, logdecay = lax.map(prepare, jnp.arange(count, dtype=jnp.int32))
    local_states, decays = jax.vmap(block_states)(inner, basis, step, logdecay)

    def pass_state(state, item):
        local, decay = item
        return (decay[:, None, None] * state + local, state)
    _, incoming = lax.scan(pass_state, jnp.zeros((MHEADS, MHEAD, STATE), jnp.float32), (local_states, decays))
    gates = gate_z.reshape(count, span, -1)

    def finish(item):
        return block_outputs(item[0], item[1], item[2], item[3], item[4], item[5], item[6], skip)
    outputs = lax.map(finish, (inner, basis, reader, step, logdecay, incoming, gates))
    return outputs.reshape(total_rows, -1)

def attend_forward(queries, keys, values, token_pos):
    count_all = queries.shape[0]
    block = math.gcd(count_all, 512)
    members = QHEADS // KVHEADS
    scale = 1.0 / math.sqrt(HEAD)
    keys_f = keys.astype(jnp.float32)
    values_f = values.astype(jnp.float32)
    key_index = jnp.arange(count_all, dtype=jnp.int32)

    def one_block(index):
        start = index * block
        rows = group_rows(lax.dynamic_slice_in_dim(queries, start, block, 0), KVHEADS).astype(jnp.float32)
        row_index = jnp.tile(start + jnp.arange(block, dtype=jnp.int32), members)
        lowest = row_index - jnp.tile(lax.dynamic_slice_in_dim(token_pos, start, block, 0), members)
        allowed = ((key_index[None, :] <= row_index[:, None]) & (key_index[None, :] >= lowest[:, None]))[None]
        scores = jnp.einsum('grd,pgd->grp', rows, keys_f) * scale
        peak = lax.optimization_barrier(jnp.max(jnp.where(allowed, scores, NEGATIVE), axis=-1))
        weights = jnp.where(allowed, jnp.exp(scores - peak[..., None]), 0.0)
        weight_sum = lax.optimization_barrier(jnp.sum(weights, axis=-1))
        rounded = lax.optimization_barrier(weights.astype(jnp.bfloat16)).astype(jnp.float32)
        accum = jnp.einsum('grp,pgd->grd', rounded, values_f)
        attended = ungroup_rows(accum / weight_sum[..., None], block).astype(jnp.bfloat16)
        return (attended, peak + jnp.log(weight_sum))
    attended, log_total = lax.map(one_block, jnp.arange(count_all // block, dtype=jnp.int32))
    return (attended.reshape(count_all, QHEADS * HEAD), log_total)

def attend_backward(queries, keys, values, token_pos, attended, log_total, attended_grad):
    count_all = queries.shape[0]
    block = math.gcd(count_all, 512)
    members = QHEADS // KVHEADS
    scale = 1.0 / math.sqrt(HEAD)
    keys_f = keys.astype(jnp.float32)
    values_f = values.astype(jnp.float32)
    key_index = jnp.arange(count_all, dtype=jnp.int32)

    def one_block(carry, item):
        key_acc, value_acc = carry
        index, block_total = item
        start = index * block
        rows = group_rows(lax.dynamic_slice_in_dim(queries, start, block, 0), KVHEADS).astype(jnp.float32)
        grad_rows = group_rows(lax.dynamic_slice_in_dim(attended_grad, start, block, 0).reshape(block, QHEADS, HEAD), KVHEADS).astype(jnp.float32)
        out_rows = group_rows(lax.dynamic_slice_in_dim(attended, start, block, 0).reshape(block, QHEADS, HEAD), KVHEADS).astype(jnp.float32)
        delta = lax.optimization_barrier(jnp.sum(grad_rows * out_rows, axis=-1))
        row_index = jnp.tile(start + jnp.arange(block, dtype=jnp.int32), members)
        lowest = row_index - jnp.tile(lax.dynamic_slice_in_dim(token_pos, start, block, 0), members)
        allowed = ((key_index[None, :] <= row_index[:, None]) & (key_index[None, :] >= lowest[:, None]))[None]
        scores = jnp.einsum('grd,pgd->grp', rows, keys_f) * scale
        probs = jnp.where(allowed, jnp.exp(scores - block_total[..., None]), 0.0)
        rounded = lax.optimization_barrier(probs.astype(jnp.bfloat16)).astype(jnp.float32)
        value_acc = value_acc + jnp.einsum('grp,grd->pgd', rounded, grad_rows)
        prob_grad = jnp.einsum('grd,pgd->grp', grad_rows, values_f)
        score_grad = lax.optimization_barrier((probs * (prob_grad - delta[..., None])).astype(jnp.bfloat16)).astype(jnp.float32)
        row_grad = jnp.einsum('grp,pgd->grd', score_grad, keys_f) * scale
        key_acc = key_acc + jnp.einsum('grp,grd->pgd', score_grad, rows) * scale
        return ((key_acc, value_acc), ungroup_rows(row_grad, block))
    zeros = jnp.zeros((count_all, KVHEADS, HEAD), jnp.float32)
    steps_index = jnp.arange(count_all // block, dtype=jnp.int32)
    (key_grad, value_grad), query_grad = lax.scan(one_block, (zeros, zeros), (steps_index, log_total))
    return (query_grad.reshape(count_all, QHEADS, HEAD), key_grad, value_grad)

def sequence_pass(tokens, token_pos, upstream, weights):
    mixer_gain, attention_in, attention_out, mamba_in, filter_taps, step_bias, decay_log, skip_gain, gated_gain, mamba_out, feed_gain, gate_weight, up_weight, down_weight = weights
    count_all = tokens.shape[0]
    mixer_f = mixer_gain.astype(jnp.float32)
    gated_f = gated_gain.astype(jnp.float32)
    feed_f = feed_gain.astype(jnp.float32)
    normed, inverse_one = rms_forward(tokens, mixer_f)
    normed_b = normed.astype(jnp.bfloat16)
    projected = matmul(normed_b, attention_in)
    cosine, sine = rotary_tables(token_pos, HEAD // 2)
    queries = rotate(projected[:, :QDIM].reshape(count_all, QHEADS, HEAD), cosine, sine).astype(jnp.bfloat16)
    keys = rotate(projected[:, QDIM:QDIM + KVDIM].reshape(count_all, KVHEADS, HEAD), cosine, sine).astype(jnp.bfloat16)
    values = projected[:, QDIM + KVDIM:].reshape(count_all, KVHEADS, HEAD).astype(jnp.bfloat16)
    queries, keys, values = lax.optimization_barrier((queries, keys, values))
    attended, log_total = attend_forward(queries, keys, values, token_pos)
    attend_branch = matmul(attended, attention_out)
    mixed = matmul(normed_b, mamba_in)
    gate_z = mixed[:, :DIN]
    conv_in = lax.optimization_barrier(mixed[:, DIN:DIN + XBC].astype(jnp.bfloat16))
    step_raw = mixed[:, DIN + XBC:]
    gated, mamba_back = jax.vjp(mamba_sequence, conv_in.astype(jnp.float32), step_raw, gate_z, filter_taps.astype(jnp.float32), step_bias.astype(jnp.float32), decay_log.astype(jnp.float32), skip_gain.astype(jnp.float32))
    mamba_normed, inverse_three = rms_forward(gated, gated_f)
    mamba_normed_b = mamba_normed.astype(jnp.bfloat16)
    middle = tokens + attend_branch + matmul(mamba_normed_b, mamba_out)
    feed_normed, inverse_two = rms_forward(middle, feed_f)
    feed_b = feed_normed.astype(jnp.bfloat16)
    gate, up, activated = feed_forward(feed_b, gate_weight, up_weight)
    hidden_out = middle + matmul(activated, down_weight)
    upstream_b = upstream.astype(jnp.bfloat16)
    gate_grad, up_grad, down_grad, feed_grad = feed_backward(feed_b, gate, up, activated, upstream_b, gate_weight, up_weight, down_weight)
    back_two, feed_gain_grad = rms_backward(middle, inverse_two, feed_f, feed_grad)
    middle_grad = upstream + back_two
    middle_b = middle_grad.astype(jnp.bfloat16)
    mamba_out_grad = matmul(mamba_normed_b.T, middle_b)
    normed_mamba_grad = matmul(middle_b, mamba_out.T)
    gated_grad, gated_gain_grad = rms_backward(gated, inverse_three, gated_f, normed_mamba_grad)
    conv_grad, raw_grad, gate_z_grad, taps_grad, bias_grad, rate_grad, skip_grad = mamba_back(gated_grad)
    mixed_grad = jnp.concatenate([gate_z_grad, conv_grad, raw_grad], axis=1).astype(jnp.bfloat16)
    mamba_in_grad = matmul(normed_b.T, mixed_grad)
    normed_grad = matmul(mixed_grad, mamba_in.T)
    attend_out_grad = matmul(attended.T, middle_b)
    attended_grad = lax.optimization_barrier(matmul(middle_b, attention_out.T).astype(jnp.bfloat16))
    query_grad, key_grad, value_grad = attend_backward(queries, keys, values, token_pos, attended, log_total, attended_grad)
    query_grad = rotate_back(query_grad, cosine, sine)
    key_grad = rotate_back(key_grad, cosine, sine)
    projected_grad = jnp.concatenate([query_grad.reshape(count_all, QDIM), key_grad.reshape(count_all, KVDIM), value_grad.reshape(count_all, KVDIM)], axis=1).astype(jnp.bfloat16)
    attend_in_grad = matmul(normed_b.T, projected_grad)
    normed_grad = normed_grad + matmul(projected_grad, attention_in.T)
    back_one, mixer_gain_grad = rms_backward(tokens, inverse_one, mixer_f, normed_grad)
    input_grad = middle_grad + back_one
    grads = (mixer_gain_grad, attend_in_grad, attend_out_grad, mamba_in_grad, taps_grad, bias_grad, rate_grad, skip_grad, gated_gain_grad, mamba_out_grad, feed_gain_grad, gate_grad, up_grad, down_grad)
    return (hidden_out, input_grad, grads)

def reference(hidden_in, positions, mixer_gain, attention_in, attention_out, mamba_in, filter_taps, step_bias, decay_log, skip_gain, gated_gain, mamba_out, feed_gain, gate_weight, up_weight, down_weight, cotangent):
    weights = (mixer_gain, attention_in, attention_out, mamba_in, filter_taps, step_bias, decay_log, skip_gain, gated_gain, mamba_out, feed_gain, gate_weight, up_weight, down_weight)
    results = [sequence_pass(hidden_in[which], positions[which], cotangent[which], weights) for which in range(NSEQ)]
    totals = results[0][2]
    for item in results[1:]:
        totals = jax.tree.map(jnp.add, totals, item[2])
    hidden_out = jnp.stack([item[0] for item in results])
    input_gradient = jnp.stack([item[1] for item in results])
    return (hidden_out, input_gradient, totals[0], totals[1], totals[2], totals[3], totals[4], totals[5], totals[6], totals[7], totals[8], totals[9], totals[10], totals[11], totals[12], totals[13])
```

```python
import functools
import math

import jax
import jax.numpy as jnp
from jax import lax
from jax.experimental import pallas as pl
from jax.experimental.pallas import tpu as pltpu
from jax.sharding import PartitionSpec as P

QHEADS = 8
KVHEADS = 2
HEAD = 64
MHEADS = 24
MHEAD = 64
STATE = 128
CONV = 4
DIN = 1536
XBC = 1792
QDIM = 512
KVDIM = 128


EPS = 1e-05
NEGATIVE = -1e30
ROPE_BASE = 10000.0
HIGH = lax.Precision.HIGHEST


BF = jnp.bfloat16
F32 = jnp.float32


def shift(value, axis, steps):
    count = lax.axis_size(axis)
    first, last = (max(0, -steps), min(count, count - steps))
    return lax.ppermute(value, axis, [(source, source + steps) for source in range(first, last)])


def swap(value, axis, bit):
    count = lax.axis_size(axis)
    return lax.ppermute(value, axis, [(source, source ^ bit) for source in range(count)])


def xor_gather(block, axis):
    held = {0: block}
    bit = lax.axis_size(axis) // 2
    while bit >= 1:
        held.update({d | bit: swap(part, axis, bit) for d, part in sorted(held.items())})
        bit //= 2
    return [held[d] for d in range(len(held))]


def xor_scatter(blocks, axis):
    held = dict(enumerate(blocks))
    bit = 1
    while bit < len(blocks):
        got = {d ^ bit: swap(held[d].astype(BF), axis, bit) for d in held if d & bit}
        held = {d: held[d].astype(F32) + got[d].astype(F32) for d in held if not d & bit}
        bit *= 2
    return held[0]


def ordered(blocks, axis):
    mine = lax.axis_index(axis)
    stack = jnp.stack(blocks)
    return [lax.dynamic_index_in_dim(stack, mine ^ j, 0, False) for j in range(len(blocks))]


def column_blocks(array, axis):
    count, mine = (lax.axis_size(axis), lax.axis_index(axis))
    width = array.shape[1] // count
    return [
        lax.dynamic_slice_in_dim(array, (mine ^ d) * width, width, 1) for d in range(count)
    ]


def carried(state, decay, axis, direction):
    count = lax.axis_size(axis)
    own_state, own_decay = (state, decay)
    out_state, out_decay = (jnp.zeros_like(state), jnp.ones_like(decay))
    step = 1
    while step < count:
        got_state = shift(own_state.astype(BF), axis, direction * step).astype(F32)
        got_decay = shift(own_decay, axis, direction * step)
        out_state = out_decay[:, None, None] * got_state + out_state
        out_decay = out_decay * got_decay
        own_state = own_decay[:, None, None] * got_state + own_state
        own_decay = own_decay * got_decay
        step *= 2
    return out_state


def matmul(left, right):
    return jnp.dot(left, right, preferred_element_type=jnp.float32)


def rms_forward(values, gain):
    inverse = lax.rsqrt(jnp.mean(values * values, axis=-1, keepdims=True) + EPS)
    return (values * inverse * gain, inverse)


def rms_backward(values, inverse, gain, upstream):
    scaled = gain * upstream
    inner = jnp.mean(scaled * values, axis=-1, keepdims=True)
    back = inverse * scaled - values * inverse**3 * inner
    return (back, jnp.sum(upstream * values * inverse, axis=0))


def mixer_inputs(window, step_raw, taps, step_bias, decay_log):
    span = step_raw.shape[0]
    convolved = taps[0] * window[0:span]
    for tap in range(1, taps.shape[0]):
        convolved = convolved + taps[tap] * window[tap : tap + span]
    activated = jax.nn.silu(convolved)
    inner = activated[:, :DIN].reshape(span, MHEADS, MHEAD)
    basis = activated[:, DIN : DIN + STATE]
    reader = activated[:, DIN + STATE :]
    step = jax.nn.softplus(step_raw + step_bias)
    logdecay = -step * jnp.exp(decay_log)
    return (inner, basis, reader, step, logdecay)


def block_states(inner, basis, step, logdecay):
    cumulative = jnp.cumsum(logdecay, axis=0)
    weight = jnp.exp(cumulative[-1][None, :] - cumulative) * step
    state = jnp.einsum("thp,tn->hpn", inner * weight[:, :, None], basis, precision=HIGH)
    return (state, jnp.exp(cumulative[-1]))


def block_outputs(inner, basis, reader, step, logdecay, incoming, gate_z, skip):
    span = step.shape[0]
    cumulative = jnp.cumsum(logdecay, axis=0)
    intersection = jnp.dot(reader, basis.T, precision=HIGH)
    order = jnp.arange(span, dtype=jnp.int32)
    causal = (order[:, None] >= order[None, :])[:, :, None]
    gap = cumulative[:, None, :] - cumulative[None, :, :]
    decay = jnp.where(causal, jnp.exp(jnp.where(causal, gap, 0.0)), 0.0)
    mixing = intersection[:, :, None] * decay * step[None, :, :]
    within = jnp.einsum("tsh,shp->thp", mixing, inner, precision=HIGH)
    carried = jnp.exp(cumulative)[:, :, None] * jnp.einsum(
        "tn,hpn->thp", reader, incoming, precision=HIGH
    )
    output = within + carried + skip[None, :, None] * inner
    return output.reshape(span, -1) * jax.nn.silu(gate_z)


def feed_forward(rows, gate_w, up_w):
    gate = matmul(rows, gate_w)
    up = matmul(rows, up_w)
    activated = (jax.nn.silu(gate) * up).astype(jnp.bfloat16)
    return (gate, up, activated)


def turned(value, lane_low):
    return jnp.where(lane_low, -pltpu.roll(value, 96, 1), pltpu.roll(value, 32, 1))


def lanes_low(rows):
    return lax.broadcasted_iota(jnp.int32, (rows, 128), 1) % HEAD < HEAD // 2


def rope_kernel(proj_ref, cos_ref, sin_ref, q_ref, kv_ref):
    rows = proj_ref.shape[0]
    low = lanes_low(rows)
    cosine, sine = (cos_ref[...], sin_ref[...])
    for j in range(QDIM // 128):
        part = proj_ref[:, j * 128 : (j + 1) * 128]
        out = part * cosine + turned(part, low) * sine
        q_ref[:, j * 128 : (j + 1) * 128] = (out.astype(BF).astype(F32) * HEAD**-0.5).astype(BF)
    part = proj_ref[:, QDIM : QDIM + KVDIM]
    keys = (part * cosine + turned(part, low) * sine).astype(BF)
    vals = proj_ref[:, QDIM + KVDIM :].astype(BF)
    for g in range(KVHEADS):
        kv_ref[:, g * 128 : g * 128 + HEAD] = keys[:, g * HEAD : (g + 1) * HEAD]
        kv_ref[:, g * 128 + HEAD : (g + 1) * 128] = vals[:, g * HEAD : (g + 1) * HEAD]


def window_bias(pos_ref, rows, span):
    row = lax.broadcasted_iota(jnp.int32, (rows, span), 0) + (span - rows)
    col = lax.broadcasted_iota(jnp.int32, (rows, span), 1)
    return (col <= row) & (col >= row - pos_ref[...])


def nt(left, right):
    return lax.dot_general(left, right, (((1,), (1,)), ((), ())), preferred_element_type=F32)


def tn(left, right):
    return lax.dot_general(left, right, (((0,), (0,)), ((), ())), preferred_element_type=F32)


def nn(left, right):
    return lax.dot_general(left, right, (((1,), (0,)), ((), ())), preferred_element_type=F32)


def attend_kernel(q_ref, kv_ref, pos_ref, o_ref, lse_ref):
    rows, span = (q_ref.shape[0], kv_ref.shape[0])
    allowed = window_bias(pos_ref, rows, span)
    keys, vals = (kv_ref[:, :HEAD], kv_ref[:, HEAD:])
    for h in range(2):
        scores = jnp.where(allowed, nt(q_ref[:, h * HEAD : (h + 1) * HEAD], keys), NEGATIVE)
        peak = jnp.max(scores, axis=1, keepdims=True)
        weights = jnp.exp(scores - peak)
        total = jnp.sum(weights, axis=1, keepdims=True)
        accum = nn(weights.astype(BF), vals)
        o_ref[:, h * HEAD : (h + 1) * HEAD] = (accum / total).astype(BF)
        lse_ref[0, :, h : h + 1] = peak + jnp.log(total)


def attend_back_kernel(q_ref, kv_ref, pos_ref, o_ref, g_ref, lse_ref, cos_ref, sin_ref, dq_ref, dkv_ref, acc_ref):
    rows, span = (q_ref.shape[0], kv_ref.shape[0])
    step = pl.program_id(0)
    per_group = QHEADS // KVHEADS // 2
    allowed = window_bias(pos_ref, rows, span)
    keys, vals = (kv_ref[:, :HEAD], kv_ref[:, HEAD:])
    out = o_ref[...].astype(F32)
    grad = g_ref[...].astype(F32)
    both = out * grad
    parts = []
    dk, dv = (None, None)
    for h in range(2):
        lanes = slice(h * HEAD, (h + 1) * HEAD)
        query, upstream = (q_ref[:, lanes], g_ref[:, lanes])
        delta = jnp.sum(both[:, lanes], axis=1, keepdims=True)
        scores = nt(query, keys)
        probs = jnp.where(allowed, jnp.exp(jnp.where(allowed, scores - lse_ref[0, :, h : h + 1], 0.0)), 0.0)
        dp = nt(upstream, vals)
        ds = (probs * (dp - delta)).astype(BF)
        parts.append(nn(ds, keys) * HEAD**-0.5)
        dk_h, dv_h = (tn(ds, query), tn(probs.astype(BF), upstream))
        dk = dk_h if dk is None else dk + dk_h
        dv = dv_h if dv is None else dv + dv_h
    low = lanes_low(rows)
    dq = jnp.concatenate(parts, axis=1)
    dq_ref[...] = (dq * cos_ref[...] - turned(dq, low) * sin_ref[...]).astype(BF)
    dkv = jnp.concatenate([dk, dv], axis=1)

    @pl.when(step % per_group == 0)
    def _():
        acc_ref[...] = dkv

    @pl.when(step % per_group != 0)
    def _():
        acc_ref[...] = acc_ref[...] + dkv

    @pl.when(step % per_group == per_group - 1)
    def _():
        dkv_ref[...] = acc_ref[...].astype(BF)


def attend(query, window, pos):
    rows, span = (query.shape[0], window.shape[0])
    pairs = QHEADS // 2
    per_group = pairs // KVHEADS
    return pl.pallas_call(
        attend_kernel,
        grid=(pairs,),
        in_specs=[
            pl.BlockSpec((rows, 128), lambda p: (0, p)),
            pl.BlockSpec((span, 128), lambda p: (0, p // per_group)),
            pl.BlockSpec((rows, 1), lambda p: (0, 0)),
        ],
        out_specs=[
            pl.BlockSpec((rows, 128), lambda p: (0, p)),
            pl.BlockSpec((1, rows, 2), lambda p: (p, 0, 0)),
        ],
        out_shape=[
            jax.ShapeDtypeStruct((rows, QDIM), BF),
            jax.ShapeDtypeStruct((pairs, rows, 2), F32),
        ],
        name="attend",
    )(query, window, pos)


def attend_back(query, window, pos, out, grad, lse, cosine, sine):
    rows, span = (query.shape[0], window.shape[0])
    pairs = QHEADS // 2
    per_group = pairs // KVHEADS
    tile = pl.BlockSpec((rows, 128), lambda p: (0, p))
    table = pl.BlockSpec((rows, 128), lambda p: (0, 0))
    wide = pl.BlockSpec((span, 128), lambda p: (0, p // per_group))
    return pl.pallas_call(
        attend_back_kernel,
        grid=(pairs,),
        in_specs=[
            tile,
            wide,
            pl.BlockSpec((rows, 1), lambda p: (0, 0)),
            tile,
            tile,
            pl.BlockSpec((1, rows, 2), lambda p: (p, 0, 0)),
            table,
            table,
        ],
        out_specs=[tile, wide],
        out_shape=[
            jax.ShapeDtypeStruct((rows, QDIM), BF),
            jax.ShapeDtypeStruct(window.shape, BF),
        ],
        scratch_shapes=[pltpu.VMEM((span, 128), F32)],
        name="attend_back",
    )(query, window, pos, out, grad, lse, cosine, sine)


def join_kernel(count, *refs):
    own_ref, rest = (refs[0], refs[1 : 1 + count])
    cos_ref, sin_ref, out_ref = refs[1 + count :]
    total = own_ref[...].astype(F32)
    for ref in rest:
        total = total + ref[...].astype(F32)
    keys = jnp.concatenate([total[:, g * 128 : g * 128 + HEAD] for g in range(KVHEADS)], axis=1)
    vals = jnp.concatenate([total[:, g * 128 + HEAD : (g + 1) * 128] for g in range(KVHEADS)], axis=1)
    back = keys * cos_ref[...] - turned(keys, lanes_low(keys.shape[0])) * sin_ref[...]
    out_ref[:, :KVDIM] = back.astype(BF)
    out_ref[:, KVDIM:] = vals.astype(BF)


def body(
    hidden_in,
    positions,
    mixer_gain,
    attention_in,
    attention_out,
    mamba_in,
    filter_taps,
    step_bias,
    decay_log,
    skip_gain,
    gated_gain,
    mamba_out,
    feed_gain,
    gate_weight,
    up_weight,
    down_weight,
    cotangent,
):
    tokens = hidden_in[0]
    token_pos = positions[0]
    upstream = cotangent[0]
    length = tokens.shape[0]
    ctx_count = lax.axis_size("ctx")
    group = lax.axis_size("fsdp")
    longest = length * ctx_count // 2
    reach = min(ctx_count - 1, (longest - 1 + length - 1) // length)

    small_parts = (
        mixer_gain,
        feed_gain,
        gated_gain,
        filter_taps.reshape(-1),
        step_bias,
        decay_log,
        skip_gain,
    )
    sizes = [part.shape[0] for part in small_parts]
    bounds = [sum(sizes[:k]) for k in range(len(sizes) + 1)]
    small = jnp.stack(ordered(xor_gather(jnp.concatenate(small_parts), "fsdp"), "fsdp"))
    mixer_f, feed_f, gated_f, taps_f, bias_f, rate_f, skip_f = (
        small[:, bounds[k] : bounds[k + 1]].astype(F32) for k in range(len(sizes))
    )
    taps_f = taps_f.reshape(group, CONV, -1).transpose(1, 0, 2).reshape(CONV, -1)
    mixer_f, feed_f, gated_f, bias_f, rate_f, skip_f = (
        part.reshape(-1) for part in (mixer_f, feed_f, gated_f, bias_f, rate_f, skip_f)
    )
    attend_in = jnp.concatenate(ordered(xor_gather(attention_in, "fsdp"), "fsdp"), axis=0)
    mamba_proj = lax.all_gather(mamba_in, "fsdp", axis=0, tiled=True)
    attend_rows = attention_out.shape[0]
    outs = lax.all_gather(jnp.concatenate([attention_out, mamba_out], axis=0), "fsdp", axis=0)
    attend_out = outs[:, :attend_rows].reshape(-1, outs.shape[-1])
    mamba_back_w = outs[:, attend_rows:].reshape(-1, outs.shape[-1])

    normed, inverse_one = rms_forward(tokens, mixer_f)
    normed_b = normed.astype(BF)
    projected = matmul(normed_b, attend_in)
    lane = jnp.arange(128, dtype=jnp.int32) % (HEAD // 2)
    frequency = jnp.exp(-math.log(ROPE_BASE) * lane.astype(F32) * (2.0 / HEAD))
    angle = token_pos.astype(F32)[:, None] * frequency[None, :]
    cosine, sine = (jnp.cos(angle), jnp.sin(angle))
    query, kv_own = pl.pallas_call(
        rope_kernel,
        out_shape=[
            jax.ShapeDtypeStruct((length, QDIM), BF),
            jax.ShapeDtypeStruct((length, 2 * KVDIM), BF),
        ],
        name="rope",
    )(projected, cosine, sine)
    window = jnp.concatenate(
        [shift(kv_own, "ctx", k) for k in range(reach, 0, -1)] + [kv_own], axis=0
    )
    pos_column = token_pos[:, None]
    attended, log_total = attend(query, window, pos_column)
    attend_branch = matmul(attended, attend_out)
    mixed = matmul(normed_b, mamba_proj)
    gate_z = mixed[:, :DIN]
    conv_in = mixed[:, DIN : DIN + XBC].astype(BF)
    step_raw = mixed[:, DIN + XBC :]
    edge = shift(conv_in[length - CONV + 1 :], "ctx", 1)
    conv_window = jnp.concatenate([edge, lax.optimization_barrier(conv_in)], axis=0).astype(F32)
    prepared, prepare_back = jax.vjp(mixer_inputs, conv_window, step_raw, taps_f, bias_f, rate_f)
    inner, basis, reader, step, logdecay = prepared
    (local_state, decay), states_back = jax.vjp(block_states, inner, basis, step, logdecay)
    incoming = carried(local_state, decay, "ctx", 1)
    gated, outputs_back = jax.vjp(
        block_outputs, inner, basis, reader, step, logdecay, incoming, gate_z, skip_f
    )
    mamba_normed, inverse_three = rms_forward(gated, gated_f)
    mamba_normed_b = mamba_normed.astype(BF)
    middle = tokens + attend_branch + matmul(mamba_normed_b, mamba_back_w)
    feed_normed, inverse_two = rms_forward(middle, feed_f)
    feed_b = feed_normed.astype(BF)
    upstream_all = jnp.concatenate(xor_gather(upstream.astype(BF), "fsdp"), axis=0)
    rows_all = jnp.concatenate(xor_gather(feed_b, "fsdp"), axis=0)

    gate, up, activated = feed_forward(rows_all, gate_weight, up_weight)
    act_grad = matmul(upstream_all, down_weight.T)
    sigma = jax.nn.sigmoid(gate)
    gate_part = (act_grad * up * sigma * (1.0 + gate * (1.0 - sigma))).astype(BF)
    up_part = (act_grad * gate * sigma).astype(BF)
    feed_back = matmul(gate_part, gate_weight.T) + matmul(up_part, up_weight.T)
    feed_grad = xor_scatter(jnp.split(feed_back, group, axis=0), "fsdp")
    feed_out = xor_scatter(jnp.split(matmul(activated, down_weight), group, axis=0), "fsdp")
    output = middle + feed_out
    feed_totals = lax.psum(
        (
            matmul(rows_all.T, gate_part).astype(BF),
            matmul(rows_all.T, up_part).astype(BF),
            matmul(activated.T, upstream_all).astype(BF),
        ),
        "ctx",
    )

    back_two, feed_gain_grad = rms_backward(middle, inverse_two, feed_f, feed_grad)
    middle_grad = upstream + back_two
    middle_b = middle_grad.astype(BF)
    out_columns = jnp.concatenate(
        [
            part
            for pair in zip(column_blocks(attended, "fsdp"), column_blocks(mamba_normed_b, "fsdp"))
            for part in pair
        ],
        axis=1,
    )
    out_grads = xor_scatter(jnp.split(matmul(out_columns.T, middle_b), group, axis=0), "fsdp")
    out_grads, feed_totals = lax.optimization_barrier((out_grads.astype(BF), feed_totals))
    out_totals = lax.psum(out_grads, "ctx")

    normed_mamba_grad = matmul(middle_b, mamba_back_w.T)
    gated_grad, gated_gain_grad = rms_backward(gated, inverse_three, gated_f, normed_mamba_grad)
    (
        grad_inner,
        grad_basis,
        grad_reader,
        grad_step,
        grad_logdecay,
        grad_incoming,
        grad_gate_z,
        skip_grad,
    ) = outputs_back(gated_grad)
    state_grad = carried(grad_incoming, decay, "ctx", -1)
    decay_grad = jnp.sum(state_grad * incoming, axis=(1, 2))
    more_inner, more_basis, more_step, more_logdecay = states_back((state_grad, decay_grad))
    window_grad, raw_grad, taps_grad, bias_grad, rate_grad = prepare_back(
        (
            grad_inner + more_inner,
            grad_basis + more_basis,
            grad_reader,
            grad_step + more_step,
            grad_logdecay + more_logdecay,
        )
    )
    returned = shift(window_grad[: CONV - 1], "ctx", -1)
    conv_grad = window_grad[CONV - 1 :]
    conv_grad = jnp.concatenate(
        [conv_grad[: length - CONV + 1], conv_grad[length - CONV + 1 :] + returned], axis=0
    )
    mixed_grad = jnp.concatenate([grad_gate_z, conv_grad, raw_grad], axis=1).astype(BF)
    normed_columns = jnp.concatenate(column_blocks(normed_b, "fsdp"), axis=1)
    mamba_in_grad = xor_scatter(
        jnp.split(matmul(normed_columns.T, mixed_grad), group, axis=0), "fsdp"
    )
    mamba_in_grad, out_totals = lax.optimization_barrier((mamba_in_grad.astype(BF), out_totals))
    mamba_in_total = lax.psum(mamba_in_grad, "ctx")
    normed_grad = matmul(mixed_grad, mamba_proj.T)

    attended_grad = matmul(middle_b, attend_out.T).astype(BF)
    query_grad, window_back = attend_back(
        query, window, pos_column, attended, attended_grad, log_total, cosine, sine
    )
    pieces = jnp.split(window_back, reach + 1, axis=0)
    kv_grad = pl.pallas_call(
        functools.partial(join_kernel, reach),
        out_shape=jax.ShapeDtypeStruct((length, 2 * KVDIM), BF),
        name="join",
    )(
        pieces[reach],
        *[shift(pieces[reach - k], "ctx", -k) for k in range(1, reach + 1)],
        cosine,
        sine,
    )
    projected_grad = jnp.concatenate([query_grad, kv_grad], axis=1)
    attend_in_grad = xor_scatter(
        jnp.split(matmul(normed_columns.T, projected_grad), group, axis=0), "fsdp"
    )
    normed_grad = normed_grad + matmul(projected_grad, attend_in.T)
    back_one, mixer_gain_grad = rms_backward(tokens, inverse_one, mixer_f, normed_grad)
    input_grad = middle_grad + back_one

    small_grads = jnp.concatenate(
        [
            mixer_gain_grad.reshape(group, -1),
            feed_gain_grad.reshape(group, -1),
            gated_gain_grad.reshape(group, -1),
            taps_grad.reshape(CONV, group, -1).transpose(1, 0, 2).reshape(group, -1),
            bias_grad.reshape(group, -1),
            rate_grad.reshape(group, -1),
            skip_grad.reshape(group, -1),
        ],
        axis=1,
    )
    mine = lax.axis_index("fsdp")
    small_own = xor_scatter(
        [lax.dynamic_index_in_dim(small_grads, mine ^ d, 0, False) for d in range(group)], "fsdp"
    )
    last, mamba_in_total = lax.optimization_barrier(
        ((attend_in_grad.astype(BF), small_own.astype(BF)), mamba_in_total)
    )
    attend_in_total, small_total = lax.psum(last, "ctx")
    total_mixer, total_feed, total_gated, total_taps, total_bias, total_rate, total_skip = (
        small_total[bounds[k] : bounds[k + 1]].astype(F32) for k in range(len(sizes))
    )
    return (
        output[None],
        input_grad[None],
        total_mixer,
        attend_in_total.astype(F32),
        out_totals[:attend_rows].astype(F32),
        mamba_in_total.astype(F32),
        total_taps.reshape(CONV, -1),
        total_bias,
        total_rate,
        total_skip,
        total_gated,
        out_totals[attend_rows:].astype(F32),
        total_feed,
        *(part.astype(F32) for part in feed_totals),
    )


def solution(mesh):
    return jax.shard_map(
        body,
        mesh=mesh,
        in_specs=(
            P("fsdp", "ctx", None),
            P("fsdp", "ctx"),
            P("fsdp"),
            P("fsdp", None),
            P("fsdp", None),
            P("fsdp", None),
            P(None, "fsdp"),
            P("fsdp"),
            P("fsdp"),
            P("fsdp"),
            P("fsdp"),
            P("fsdp", None),
            P("fsdp"),
            P(None, "fsdp"),
            P(None, "fsdp"),
            P("fsdp", None),
            P("fsdp", "ctx", None),
        ),
        out_specs=(
            P("fsdp", "ctx", None),
            P("fsdp", "ctx", None),
            P("fsdp"),
            P("fsdp", None),
            P("fsdp", None),
            P("fsdp", None),
            P(None, "fsdp"),
            P("fsdp"),
            P("fsdp"),
            P("fsdp"),
            P("fsdp"),
            P("fsdp", None),
            P("fsdp"),
            P(None, "fsdp"),
            P(None, "fsdp"),
            P("fsdp", None),
        ),
        check_vma=False,
    )
```

```python
import functools
import math

import jax
import jax.numpy as jnp
from jax import lax
from jax.experimental import pallas as pl
from jax.experimental.pallas import tpu as pltpu
from jax.sharding import PartitionSpec as P

QHEADS = 8
KVHEADS = 2
HEAD = 64
MHEADS = 24
MHEAD = 64
STATE = 128
CONV = 4
DIN = 1536
XBC = 1792
QDIM = 512
KVDIM = 128


EPS = 1e-05
NEGATIVE = -1e30
ROPE_BASE = 10000.0
HIGH = lax.Precision.HIGHEST


BF = jnp.bfloat16
F32 = jnp.float32


def shift(value, axis, steps):
    count = lax.axis_size(axis)
    first, last = (max(0, -steps), min(count, count - steps))
    return lax.ppermute(value, axis, [(source, source + steps) for source in range(first, last)])


def swap(value, axis, bit):
    count = lax.axis_size(axis)
    return lax.ppermute(value, axis, [(source, source ^ bit) for source in range(count)])


def xor_gather(block, axis):
    held = {0: block}
    bit = lax.axis_size(axis) // 2
    while bit >= 1:
        held.update({d | bit: swap(part, axis, bit) for d, part in sorted(held.items())})
        bit //= 2
    return [held[d] for d in range(len(held))]


def xor_scatter(blocks, axis):
    held = dict(enumerate(blocks))
    bit = 1
    while bit < len(blocks):
        got = {d ^ bit: swap(held[d].astype(BF), axis, bit) for d in held if d & bit}
        held = {d: held[d].astype(F32) + got[d].astype(F32) for d in held if not d & bit}
        bit *= 2
    return held[0]


def ordered(blocks, axis):
    mine = lax.axis_index(axis)
    stack = jnp.stack(blocks)
    return [lax.dynamic_index_in_dim(stack, mine ^ j, 0, False) for j in range(len(blocks))]


def column_blocks(array, axis):
    count, mine = (lax.axis_size(axis), lax.axis_index(axis))
    width = array.shape[1] // count
    return [
        lax.dynamic_slice_in_dim(array, (mine ^ d) * width, width, 1) for d in range(count)
    ]


def all_sum(array, axis, turn=0):
    mine = lax.axis_index(axis)
    bits = [1 << k for k in range((lax.axis_size(axis) - 1).bit_length())]
    bits = bits[turn:] + bits[:turn]
    for bit in bits:
        high = (mine & bit) != 0
        low_half, high_half = jnp.split(array, 2, axis=0)
        got = swap(jnp.where(high, low_half, high_half).astype(BF), axis, bit)
        array = jnp.where(high, high_half, low_half).astype(F32) + got.astype(F32)
    array = array.astype(BF)
    for bit in reversed(bits):
        high = (mine & bit) != 0
        got = swap(array, axis, bit)
        array = jnp.where(
            high, jnp.concatenate([got, array], axis=0), jnp.concatenate([array, got], axis=0)
        )
    return array


def carried(state, decay, axis, direction):
    count = lax.axis_size(axis)
    own_state, own_decay = (state, decay)
    out_state, out_decay = (jnp.zeros_like(state), jnp.ones_like(decay))
    step = 1
    while step < count:
        got_state = shift(own_state.astype(BF), axis, direction * step).astype(F32)
        got_decay = shift(own_decay, axis, direction * step)
        out_state = jnp.repeat(out_decay, MHEAD)[:, None] * got_state + out_state
        out_decay = out_decay * got_decay
        own_state = jnp.repeat(own_decay, MHEAD)[:, None] * got_state + own_state
        own_decay = own_decay * got_decay
        step *= 2
    return out_state


def matmul(left, right):
    return jnp.dot(left, right, preferred_element_type=jnp.float32)


def rms_forward(values, gain):
    inverse = lax.rsqrt(jnp.mean(values * values, axis=-1, keepdims=True) + EPS)
    return (values * inverse * gain, inverse)


def rms_backward(values, inverse, gain, upstream):
    scaled = gain * upstream
    inner = jnp.mean(scaled * values, axis=-1, keepdims=True)
    back = inverse * scaled - values * inverse**3 * inner
    return (back, jnp.sum(upstream * values * inverse, axis=0))


def feed_forward(rows, gate_w, up_w):
    gate = matmul(rows, gate_w)
    up = matmul(rows, up_w)
    activated = (jax.nn.silu(gate) * up).astype(jnp.bfloat16)
    return (gate, up, activated)


def turned(value, lane_low):
    return jnp.where(lane_low, -pltpu.roll(value, 96, 1), pltpu.roll(value, 32, 1))


def lanes_low(rows):
    return lax.broadcasted_iota(jnp.int32, (rows, 128), 1) % HEAD < HEAD // 2


def rope_kernel(proj_ref, cos_ref, sin_ref, q_ref, kv_ref):
    rows = proj_ref.shape[0]
    low = lanes_low(rows)
    cosine, sine = (cos_ref[...], sin_ref[...])
    for j in range(QDIM // 128):
        part = proj_ref[:, j * 128 : (j + 1) * 128]
        out = part * cosine + turned(part, low) * sine
        q_ref[:, j * 128 : (j + 1) * 128] = (out.astype(BF).astype(F32) * HEAD**-0.5).astype(BF)
    part = proj_ref[:, QDIM : QDIM + KVDIM]
    keys = (part * cosine + turned(part, low) * sine).astype(BF)
    vals = proj_ref[:, QDIM + KVDIM :].astype(BF)
    for g in range(KVHEADS):
        kv_ref[:, g * 128 : g * 128 + HEAD] = keys[:, g * HEAD : (g + 1) * HEAD]
        kv_ref[:, g * 128 + HEAD : (g + 1) * 128] = vals[:, g * HEAD : (g + 1) * HEAD]


def window_bias(pos_ref, rows, span):
    row = lax.broadcasted_iota(jnp.int32, (rows, span), 0) + (span - rows)
    col = lax.broadcasted_iota(jnp.int32, (rows, span), 1)
    return (col <= row) & (col >= row - pos_ref[...])


def nt(left, right):
    return lax.dot_general(left, right, (((1,), (1,)), ((), ())), preferred_element_type=F32)


def tn(left, right):
    return lax.dot_general(left, right, (((0,), (0,)), ((), ())), preferred_element_type=F32)


def nn(left, right):
    return lax.dot_general(left, right, (((1,), (0,)), ((), ())), preferred_element_type=F32)


def attend_kernel(q_ref, kv_ref, pos_ref, o_ref, lse_ref):
    rows, span = (q_ref.shape[0], kv_ref.shape[0])
    allowed = window_bias(pos_ref, rows, span)
    keys, vals = (kv_ref[:, :HEAD], kv_ref[:, HEAD:])
    for h in range(2):
        scores = jnp.where(allowed, nt(q_ref[:, h * HEAD : (h + 1) * HEAD], keys), NEGATIVE)
        peak = jnp.max(scores, axis=1, keepdims=True)
        weights = jnp.exp(scores - peak)
        total = jnp.sum(weights, axis=1, keepdims=True)
        accum = nn(weights.astype(BF), vals)
        o_ref[:, h * HEAD : (h + 1) * HEAD] = (accum / total).astype(BF)
        lse_ref[0, :, h : h + 1] = peak + jnp.log(total)


def attend_back_kernel(q_ref, kv_ref, pos_ref, o_ref, g_ref, lse_ref, cos_ref, sin_ref, dq_ref, dkv_ref, acc_ref):
    rows, span = (q_ref.shape[0], kv_ref.shape[0])
    step = pl.program_id(0)
    per_group = QHEADS // KVHEADS // 2
    allowed = window_bias(pos_ref, rows, span)
    keys, vals = (kv_ref[:, :HEAD], kv_ref[:, HEAD:])
    out = o_ref[...].astype(F32)
    grad = g_ref[...].astype(F32)
    both = out * grad
    parts = []
    dk, dv = (None, None)
    for h in range(2):
        lanes = slice(h * HEAD, (h + 1) * HEAD)
        query, upstream = (q_ref[:, lanes], g_ref[:, lanes])
        delta = jnp.sum(both[:, lanes], axis=1, keepdims=True)
        scores = nt(query, keys)
        probs = jnp.where(allowed, jnp.exp(jnp.where(allowed, scores - lse_ref[0, :, h : h + 1], 0.0)), 0.0)
        dp = nt(upstream, vals)
        ds = (probs * (dp - delta)).astype(BF)
        parts.append(nn(ds, keys) * HEAD**-0.5)
        dk_h, dv_h = (tn(ds, query), tn(probs.astype(BF), upstream))
        dk = dk_h if dk is None else dk + dk_h
        dv = dv_h if dv is None else dv + dv_h
    low = lanes_low(rows)
    dq = jnp.concatenate(parts, axis=1)
    dq_ref[...] = (dq * cos_ref[...] - turned(dq, low) * sin_ref[...]).astype(BF)
    dkv = jnp.concatenate([dk, dv], axis=1)

    @pl.when(step % per_group == 0)
    def _():
        acc_ref[...] = dkv

    @pl.when(step % per_group != 0)
    def _():
        acc_ref[...] = acc_ref[...] + dkv

    @pl.when(step % per_group == per_group - 1)
    def _():
        dkv_ref[...] = acc_ref[...].astype(BF)


def attend(query, window, pos):
    rows, span = (query.shape[0], window.shape[0])
    pairs = QHEADS // 2
    per_group = pairs // KVHEADS
    return pl.pallas_call(
        attend_kernel,
        grid=(pairs,),
        in_specs=[
            pl.BlockSpec((rows, 128), lambda p: (0, p)),
            pl.BlockSpec((span, 128), lambda p: (0, p // per_group)),
            pl.BlockSpec((rows, 1), lambda p: (0, 0)),
        ],
        out_specs=[
            pl.BlockSpec((rows, 128), lambda p: (0, p)),
            pl.BlockSpec((1, rows, 2), lambda p: (p, 0, 0)),
        ],
        out_shape=[
            jax.ShapeDtypeStruct((rows, QDIM), BF),
            jax.ShapeDtypeStruct((pairs, rows, 2), F32),
        ],
        name="attend",
    )(query, window, pos)


def attend_back(query, window, pos, out, grad, lse, cosine, sine):
    rows, span = (query.shape[0], window.shape[0])
    pairs = QHEADS // 2
    per_group = pairs // KVHEADS
    tile = pl.BlockSpec((rows, 128), lambda p: (0, p))
    table = pl.BlockSpec((rows, 128), lambda p: (0, 0))
    wide = pl.BlockSpec((span, 128), lambda p: (0, p // per_group))
    return pl.pallas_call(
        attend_back_kernel,
        grid=(pairs,),
        in_specs=[
            tile,
            wide,
            pl.BlockSpec((rows, 1), lambda p: (0, 0)),
            tile,
            tile,
            pl.BlockSpec((1, rows, 2), lambda p: (p, 0, 0)),
            table,
            table,
        ],
        out_specs=[tile, wide],
        out_shape=[
            jax.ShapeDtypeStruct((rows, QDIM), BF),
            jax.ShapeDtypeStruct(window.shape, BF),
        ],
        scratch_shapes=[pltpu.VMEM((span, 128), F32)],
        name="attend_back",
    )(query, window, pos, out, grad, lse, cosine, sine)


def join_kernel(count, *refs):
    own_ref, rest = (refs[0], refs[1 : 1 + count])
    cos_ref, sin_ref, out_ref = refs[1 + count :]
    total = own_ref[...].astype(F32)
    for ref in rest:
        total = total + ref[...].astype(F32)
    keys = jnp.concatenate([total[:, g * 128 : g * 128 + HEAD] for g in range(KVHEADS)], axis=1)
    vals = jnp.concatenate([total[:, g * 128 + HEAD : (g + 1) * 128] for g in range(KVHEADS)], axis=1)
    back = keys * cos_ref[...] - turned(keys, lanes_low(keys.shape[0])) * sin_ref[...]
    out_ref[:, :KVDIM] = back.astype(BF)
    out_ref[:, KVDIM:] = vals.astype(BF)


def sigmoid(value):
    return 1.0 / (1.0 + jnp.exp(-value))


def pick(array, lane):
    lanes = lax.broadcasted_iota(jnp.int32, array.shape, 1)
    return jnp.sum(jnp.where(lanes == lane, array, 0.0), axis=1, keepdims=True)


def spread(pair, rows):
    lanes = lax.broadcasted_iota(jnp.int32, (rows, 128), 1)
    return jnp.where(lanes < MHEAD, pair[0], pair[1])


def halves(value):
    return [jnp.sum(value[:, h * MHEAD : (h + 1) * MHEAD], axis=1, keepdims=True) for h in range(2)]


def triangle(rows, lower):
    row = lax.broadcasted_iota(jnp.int32, (rows, rows), 0)
    col = lax.broadcasted_iota(jnp.int32, (rows, rows), 1)
    return row >= col if lower else row <= col


def exact(left, right, dims):
    return lax.dot_general(left, right, ((dims[0], dims[1]), ((), ())), precision=HIGH, preferred_element_type=F32)


def prep_kernel(raw_ref, bias_ref, rate_ref, step_ref, cum_ref, cum_rows_ref):
    rows = raw_ref.shape[0]
    value = raw_ref[...] + bias_ref[...]
    step = jnp.maximum(value, 0.0) + jnp.log1p(jnp.exp(-jnp.abs(value)))
    logdecay = -step * jnp.exp(rate_ref[...])
    step_ref[...] = step
    cum_ref[...] = exact(triangle(rows, True).astype(F32), logdecay, ((1,), (0,)))
    cum_rows_ref[...] = exact(logdecay, triangle(rows, False).astype(F32), ((0,), (0,)))


def shifted_rows(mixed_ref, edge_ref):
    rows = mixed_ref.shape[0]
    full = jnp.concatenate([edge_ref[...].astype(F32), mixed_ref[...].astype(BF).astype(F32)], axis=0)
    first = edge_ref.shape[0] - CONV + 1
    return [full[first + k : first + k + rows] for k in range(CONV)]


def convolve(views, taps_ref):
    total = taps_ref[0:1, :] * views[0]
    for k in range(1, CONV):
        total = total + taps_ref[k : k + 1, :] * views[k]
    return total


def conv_kernel(mixed_ref, edge_ref, taps_ref, act_ref):
    value = convolve(shifted_rows(mixed_ref, edge_ref), taps_ref)
    act_ref[...] = value * sigmoid(value)


def decay_matrix(cum, cum_rows_ref, head):
    rows = cum.shape[0]
    causal = triangle(rows, True)
    gap = pick(cum, head) - cum_rows_ref[pl.ds(head, 1), :]
    return jnp.where(causal, jnp.exp(jnp.where(causal, gap, 0.0)), 0.0)


def scan_kernel(x_ref, b_ref, c_ref, step_ref, cum_ref, cum_rows_ref, skip_ref, y_ref, state_ref, mix_ref):
    pair = pl.program_id(0)
    rows = x_ref.shape[0]
    basis = b_ref[...].astype(BF)

    @pl.when(pair == 0)
    def _():
        mix_ref[...] = nt(c_ref[...].astype(BF), basis)

    cum, step = (cum_ref[...], step_ref[...])
    inner = x_ref[...]
    steps = [pick(step, 2 * pair + h) for h in range(2)]
    cums = [pick(cum, 2 * pair + h) for h in range(2)]
    last = cum_ref[rows - 1 : rows, :]
    lasts = [pick(last, 2 * pair + h) for h in range(2)]
    scaled = inner * spread(steps, rows)
    scaled_b = scaled.astype(BF)
    weighted = scaled * spread([jnp.exp(lasts[h] - cums[h]) for h in range(2)], rows)
    state_ref[...] = tn(weighted.astype(BF), basis)
    parts = []
    for h in range(2):
        mixing = mix_ref[...] * decay_matrix(cum, cum_rows_ref, 2 * pair + h)
        parts.append(nn(mixing.astype(BF), scaled_b[:, h * MHEAD : (h + 1) * MHEAD]))
    y_ref[...] = jnp.concatenate(parts, axis=1) + skip_ref[...] * inner


def finish_kernel(y_ref, z_ref, c_ref, cum_ref, in_ref, gain_ref, out_y_ref, out_ref, inverse_ref):
    rows = y_ref.shape[0]
    reader = c_ref[...].astype(BF)
    growth = jnp.exp(cum_ref[...])
    square = jnp.zeros((rows, 1), F32)
    pairs = y_ref.shape[1] // 128
    for j in range(pairs):
        cols = slice(j * 128, (j + 1) * 128)
        carry = nt(reader, in_ref[cols, :].astype(BF))
        grow = spread([growth[:, 2 * j + h : 2 * j + h + 1] for h in range(2)], rows)
        total = y_ref[:, cols] + grow * carry
        out_y_ref[:, cols] = total
        gate = z_ref[:, cols]
        gated = total * (gate * sigmoid(gate))
        square = square + jnp.sum(gated * gated, axis=1, keepdims=True)
    inverse = lax.rsqrt(square / y_ref.shape[1] + EPS)
    inverse_ref[...] = inverse
    for j in range(pairs):
        cols = slice(j * 128, (j + 1) * 128)
        gate = z_ref[:, cols]
        gated = out_y_ref[:, cols] * (gate * sigmoid(gate))
        out_ref[:, cols] = (gated * inverse * gain_ref[:, cols]).astype(BF)


def gate_back_kernel(up_ref, y_ref, z_ref, c_ref, cum_ref, gain_ref, inverse_ref, dy_ref, dz_ref, din_ref, dgain_ref):
    rows = y_ref.shape[0]
    reader = c_ref[...].astype(BF)
    growth = jnp.exp(cum_ref[...])
    inverse = inverse_ref[...]
    pairs = y_ref.shape[1] // 128
    inside = jnp.zeros((rows, 1), F32)
    for j in range(pairs):
        cols = slice(j * 128, (j + 1) * 128)
        gate = z_ref[:, cols]
        gated = y_ref[:, cols] * (gate * sigmoid(gate))
        product = up_ref[:, cols] * gated
        dgain_ref[:, cols] = jnp.sum(product * inverse, axis=0, keepdims=True)
        inside = inside + jnp.sum(product * gain_ref[:, cols], axis=1, keepdims=True)
    factor = inverse * inverse * inverse * (inside / y_ref.shape[1])
    for j in range(pairs):
        cols = slice(j * 128, (j + 1) * 128)
        gate = z_ref[:, cols]
        sigma = sigmoid(gate)
        scan = y_ref[:, cols]
        back = inverse * gain_ref[:, cols] * up_ref[:, cols] - scan * (gate * sigma) * factor
        dy = back * (gate * sigma)
        dy_ref[:, cols] = dy
        dz_ref[:, cols] = (back * scan * sigma * (1.0 + gate * (1.0 - sigma))).astype(BF)
        grow = spread([growth[:, 2 * j + h : 2 * j + h + 1] for h in range(2)], rows)
        din_ref[cols, :] = tn((dy * grow).astype(BF), reader)


def scan_back_kernel(
    x_ref, b_ref, c_ref, step_ref, cum_ref, cum_rows_ref, skip_ref, y_ref, dy_ref, in_ref,
    dx_ref, dbc_ref, dstep_ref, dcum_ref, dskip_ref, mix_ref, dmix_ref, dc_ref,
):
    pair = pl.program_id(0)
    rows = x_ref.shape[0]

    @pl.when(pair == 0)
    def _():
        mix_ref[...] = nt(c_ref[...].astype(BF), b_ref[...].astype(BF))
        dmix_ref[...] = jnp.zeros(dmix_ref.shape, F32)
        dc_ref[...] = jnp.zeros(dc_ref.shape, F32)
        dstep_ref[...] = jnp.zeros(dstep_ref.shape, F32)
        dcum_ref[...] = jnp.zeros(dcum_ref.shape, F32)

    cum, step = (cum_ref[...], step_ref[...])
    inner, dy, skip = (x_ref[...], dy_ref[...], skip_ref[...])
    steps = spread([pick(step, 2 * pair + h) for h in range(2)], rows)
    grow = spread([jnp.exp(pick(cum, 2 * pair + h)) for h in range(2)], rows)
    scaled_b, dy_b = ((inner * steps).astype(BF), dy.astype(BF))
    dc_ref[...] += nn((dy * grow).astype(BF), in_ref[...].astype(BF))
    parts = []
    for h in range(2):
        lanes = slice(h * MHEAD, (h + 1) * MHEAD)
        decay = decay_matrix(cum, cum_rows_ref, 2 * pair + h)
        parts.append(tn((mix_ref[...] * decay).astype(BF), dy_b[:, lanes]))
        dmix_ref[...] += nt(dy_b[:, lanes], scaled_b[:, lanes]) * decay
    back = jnp.concatenate(parts, axis=1)
    dx_ref[...] = back * steps + skip * dy
    dsteps = halves(back * inner)
    stays = halves(dy * (y_ref[...] - skip * inner))
    lane = lax.broadcasted_iota(jnp.int32, dstep_ref.shape, 1)
    for h in range(2):
        here = lane == 2 * pair + h
        column = pick(step, 2 * pair + h)
        dstep_ref[...] += jnp.where(here, dsteps[h], 0.0)
        dcum_ref[...] += jnp.where(here, stays[h] - column * dsteps[h], 0.0)
    dskip_ref[...] = jnp.sum(dy * inner, axis=0, keepdims=True)

    @pl.when(pair == pl.num_programs(0) - 1)
    def _():
        dmix = dmix_ref[...].astype(BF)
        dbc_ref[:, :STATE] = tn(dmix, c_ref[...].astype(BF))
        dbc_ref[:, STATE:] = dc_ref[...] + nn(dmix, b_ref[...].astype(BF))


def conv_back_kernel(
    mixed_ref, edge_ref, taps_ref, x_ref, b_ref, dx_ref, dbc_ref, dstate_ref, in_ref, step_ref, cum_ref,
    dstep_in_ref, dcum_in_ref,
    dconv_ref, head_ref, dtaps_ref, dstep_ref, dcum_ref, dact_ref, db_ref,
):
    block = pl.program_id(0)
    rows = x_ref.shape[0]
    pairs = pl.num_programs(0) - 2

    @pl.when(block == 0)
    def _():
        db_ref[...] = dbc_ref[:, :STATE]
        dstep_ref[...] = dstep_in_ref[...]
        dcum_ref[...] = dcum_in_ref[...]

    @pl.when(block < pairs)
    def _():
        cum, step = (cum_ref[...], step_ref[...])
        inner = x_ref[...]
        last = cum_ref[rows - 1 : rows, :]
        lane = lax.broadcasted_iota(jnp.int32, step.shape, 1)
        row = lax.broadcasted_iota(jnp.int32, step.shape, 0)
        fades = [jnp.exp(pick(last, 2 * block + h) - pick(cum, 2 * block + h)) for h in range(2)]
        steps = [pick(step, 2 * block + h) for h in range(2)]
        weight = spread([fades[h] * steps[h] for h in range(2)], rows)
        dstate = dstate_ref[...]
        dstate_b = dstate.astype(BF)
        back = nt(b_ref[...].astype(BF), dstate_b)
        db_ref[...] += nn((inner * weight).astype(BF), dstate_b)
        dact_ref[...] = dx_ref[...] + weight * back
        dweights = halves(inner * back)
        passed = dstate * in_ref[...]
        for h in range(2):
            here = lane == 2 * block + h
            moved = fades[h] * steps[h] * dweights[h]
            decay = jnp.exp(pick(last, 2 * block + h))
            lanes = slice(h * MHEAD, (h + 1) * MHEAD)
            end = jnp.sum(moved) + jnp.sum(passed[lanes, :]) * decay
            dstep_ref[...] += jnp.where(here, fades[h] * dweights[h], 0.0)
            dcum_ref[...] += jnp.where(here, jnp.where(row == rows - 1, end, 0.0) - moved, 0.0)

    @pl.when(block == pairs)
    def _():
        dact_ref[...] = db_ref[...]

    @pl.when(block == pairs + 1)
    def _():
        dact_ref[...] = dbc_ref[:, STATE:]

    views = shifted_rows(mixed_ref, edge_ref)
    value = convolve(views, taps_ref)
    sigma = sigmoid(value)
    dvalue = dact_ref[...] * sigma * (1.0 + value * (1.0 - sigma))
    for k in range(CONV):
        dtaps_ref[k : k + 1, :] = jnp.sum(dvalue * views[k], axis=0, keepdims=True)
    pad = head_ref.shape[0]
    padding = jnp.zeros((pad, 128), F32)
    padded = jnp.concatenate([padding, dvalue, padding], axis=0)
    total = None
    for k in range(CONV):
        term = taps_ref[k : k + 1, :] * padded[CONV - 1 - k : CONV - 1 - k + rows + pad]
        total = term if total is None else total + term
    head_ref[...] = total[:pad]
    dconv_ref[...] = total[pad:]


def step_back_kernel(raw_ref, bias_ref, rate_ref, step_ref, dstep_ref, dcum_ref, draw_ref, dbias_ref, drate_ref):
    rows = raw_ref.shape[0]
    rate = jnp.exp(rate_ref[...])
    dlog = exact(triangle(rows, False).astype(F32), dcum_ref[...], ((1,), (0,)))
    draw = (dstep_ref[...] - dlog * rate) * sigmoid(raw_ref[...] + bias_ref[...])
    draw_ref[...] = draw
    dbias_ref[...] = jnp.sum(draw, axis=0, keepdims=True)
    drate_ref[...] = jnp.sum(-dlog * step_ref[...] * rate, axis=0, keepdims=True)


def whole(shape):
    return pl.BlockSpec(shape, lambda j: (0,) * len(shape))


def columns(rows, first=0):
    return pl.BlockSpec((rows, 128), lambda j: (0, first + j))


def fixed(rows, index):
    return pl.BlockSpec((rows, 128), lambda j: (0, index))


PAIRS = DIN // 128
BLOCKS = XBC // 128


def struct(*shape, dtype=F32):
    return jax.ShapeDtypeStruct(shape, dtype)


def mamba_prep(raw, bias, rate):
    rows = raw.shape[0]
    return pl.pallas_call(
        prep_kernel,
        out_shape=[struct(rows, MHEADS), struct(rows, MHEADS), struct(MHEADS, rows)],
        name="prep",
    )(raw, bias, rate)


def mamba_conv(mixed, edge, taps):
    rows = mixed.shape[0]
    return pl.pallas_call(
        conv_kernel,
        grid=(BLOCKS,),
        in_specs=[columns(rows, PAIRS), columns(edge.shape[0]), columns(CONV)],
        out_specs=columns(rows),
        out_shape=struct(rows, XBC),
        name="conv",
    )(mixed, edge, taps)


def mamba_scan(act, step, cum, cum_rows, skip):
    rows = act.shape[0]
    return pl.pallas_call(
        scan_kernel,
        grid=(PAIRS,),
        in_specs=[
            columns(rows),
            fixed(rows, PAIRS),
            fixed(rows, PAIRS + 1),
            whole(step.shape),
            whole(cum.shape),
            whole(cum_rows.shape),
            columns(1),
        ],
        out_specs=[columns(rows), pl.BlockSpec((128, STATE), lambda j: (j, 0))],
        out_shape=[struct(rows, DIN), struct(DIN, STATE)],
        scratch_shapes=[pltpu.VMEM((rows, rows), F32)],
        name="scan",
    )(act, act, act, step, cum, cum_rows, skip)


def mamba_finish(y_local, mixed, act, cum, incoming, gain):
    rows = act.shape[0]
    return pl.pallas_call(
        finish_kernel,
        grid=(1,),
        in_specs=[
            whole(y_local.shape),
            whole((rows, DIN)),
            fixed(rows, PAIRS + 1),
            whole(cum.shape),
            whole(incoming.shape),
            whole(gain.shape),
        ],
        out_specs=[whole((rows, DIN)), whole((rows, DIN)), whole((rows, 1))],
        out_shape=[struct(rows, DIN), struct(rows, DIN, dtype=BF), struct(rows, 1)],
        name="finish",
    )(y_local, mixed, act, cum, incoming, gain)


def mamba_gate_back(grad, y, mixed, act, cum, gain, inverse):
    rows = act.shape[0]
    return pl.pallas_call(
        gate_back_kernel,
        grid=(1,),
        in_specs=[
            whole((rows, DIN)),
            whole((rows, DIN)),
            whole((rows, DIN)),
            fixed(rows, PAIRS + 1),
            whole(cum.shape),
            whole(gain.shape),
            whole((rows, 1)),
        ],
        out_specs=[whole((rows, DIN)), whole((rows, DIN)), whole((DIN, STATE)), whole((1, DIN))],
        out_shape=[struct(rows, DIN), struct(rows, DIN, dtype=BF), struct(DIN, STATE), struct(1, DIN)],
        name="gate_back",
    )(grad, y, mixed, act, cum, gain, inverse)


def mamba_scan_back(act, step, cum, cum_rows, skip, y, dy, incoming):
    rows = act.shape[0]
    return pl.pallas_call(
        scan_back_kernel,
        grid=(PAIRS,),
        in_specs=[
            columns(rows),
            fixed(rows, PAIRS),
            fixed(rows, PAIRS + 1),
            whole(step.shape),
            whole(cum.shape),
            whole(cum_rows.shape),
            columns(1),
            columns(rows),
            columns(rows),
            pl.BlockSpec((128, STATE), lambda j: (j, 0)),
        ],
        out_specs=[columns(rows), whole((rows, 2 * STATE)), whole(step.shape), whole(step.shape), columns(1)],
        out_shape=[
            struct(rows, DIN),
            struct(rows, 2 * STATE),
            struct(*step.shape),
            struct(*step.shape),
            struct(1, DIN),
        ],
        scratch_shapes=[
            pltpu.VMEM((rows, rows), F32),
            pltpu.VMEM((rows, rows), F32),
            pltpu.VMEM((rows, STATE), F32),
        ],
        name="scan_back",
    )(act, act, act, step, cum, cum_rows, skip, y, dy, incoming)


def mamba_conv_back(mixed, edge, taps, act, dx, dbc, dstate, incoming, step, cum, dstep, dcum):
    rows = act.shape[0]
    pad = edge.shape[0]
    clipped = pl.BlockSpec((rows, 128), lambda j: (0, jnp.minimum(j, PAIRS - 1)))
    states = pl.BlockSpec((128, STATE), lambda j: (jnp.minimum(j, PAIRS - 1), 0))
    return pl.pallas_call(
        conv_back_kernel,
        grid=(BLOCKS,),
        in_specs=[
            columns(rows, PAIRS),
            columns(pad),
            columns(CONV),
            clipped,
            fixed(rows, PAIRS),
            clipped,
            whole(dbc.shape),
            states,
            states,
            whole(step.shape),
            whole(step.shape),
            whole(step.shape),
            whole(step.shape),
        ],
        out_specs=[columns(rows), columns(pad), columns(CONV), whole(step.shape), whole(step.shape)],
        out_shape=[
            struct(rows, XBC),
            struct(pad, XBC),
            struct(CONV, XBC),
            struct(*step.shape),
            struct(*step.shape),
        ],
        scratch_shapes=[pltpu.VMEM((rows, 128), F32), pltpu.VMEM((rows, STATE), F32)],
        name="conv_back",
    )(mixed, edge, taps, act, act, dx, dbc, dstate, incoming, step, cum, dstep, dcum)


def mamba_step_back(raw, bias, rate, step, dstep, dcum):
    return pl.pallas_call(
        step_back_kernel,
        out_shape=[struct(*raw.shape), struct(1, MHEADS), struct(1, MHEADS)],
        name="step_back",
    )(raw, bias, rate, step, dstep, dcum)


def body(
    hidden_in,
    positions,
    mixer_gain,
    attention_in,
    attention_out,
    mamba_in,
    filter_taps,
    step_bias,
    decay_log,
    skip_gain,
    gated_gain,
    mamba_out,
    feed_gain,
    gate_weight,
    up_weight,
    down_weight,
    cotangent,
):
    tokens = hidden_in[0]
    token_pos = positions[0]
    upstream = cotangent[0]
    length = tokens.shape[0]
    ctx_count = lax.axis_size("ctx")
    group = lax.axis_size("fsdp")
    longest = length * ctx_count // 2
    reach = min(ctx_count - 1, (longest - 1 + length - 1) // length)

    small_parts = (
        mixer_gain,
        feed_gain,
        gated_gain,
        filter_taps.reshape(-1),
        step_bias,
        decay_log,
        skip_gain,
    )
    sizes = [part.shape[0] for part in small_parts]
    bounds = [sum(sizes[:k]) for k in range(len(sizes) + 1)]
    small = jnp.stack(ordered(xor_gather(jnp.concatenate(small_parts), "fsdp"), "fsdp"))
    mixer_f, feed_f, gated_f, taps_f, bias_f, rate_f, skip_f = (
        small[:, bounds[k] : bounds[k + 1]].astype(F32) for k in range(len(sizes))
    )
    taps_f = taps_f.reshape(group, CONV, -1).transpose(1, 0, 2).reshape(CONV, -1)
    mixer_f, feed_f, gated_f, bias_f, rate_f, skip_f = (
        part.reshape(-1) for part in (mixer_f, feed_f, gated_f, bias_f, rate_f, skip_f)
    )
    attend_in = jnp.concatenate(ordered(xor_gather(attention_in, "fsdp"), "fsdp"), axis=0)
    mamba_proj = lax.all_gather(mamba_in, "fsdp", axis=0, tiled=True)
    attend_rows = attention_out.shape[0]
    outs = lax.all_gather(jnp.concatenate([attention_out, mamba_out], axis=0), "fsdp", axis=0)
    attend_out = outs[:, :attend_rows].reshape(-1, outs.shape[-1])
    mamba_back_w = outs[:, attend_rows:].reshape(-1, outs.shape[-1])

    normed, inverse_one = rms_forward(tokens, mixer_f)
    normed_b = normed.astype(BF)
    projected = matmul(normed_b, attend_in)
    lane = jnp.arange(128, dtype=jnp.int32) % (HEAD // 2)
    frequency = jnp.exp(-math.log(ROPE_BASE) * lane.astype(F32) * (2.0 / HEAD))
    angle = token_pos.astype(F32)[:, None] * frequency[None, :]
    cosine, sine = (jnp.cos(angle), jnp.sin(angle))
    query, kv_own = pl.pallas_call(
        rope_kernel,
        out_shape=[
            jax.ShapeDtypeStruct((length, QDIM), BF),
            jax.ShapeDtypeStruct((length, 2 * KVDIM), BF),
        ],
        name="rope",
    )(projected, cosine, sine)
    window = jnp.concatenate(
        [shift(kv_own, "ctx", k) for k in range(reach, 0, -1)] + [kv_own], axis=0
    )
    pos_column = token_pos[:, None]
    upstream_all = jnp.concatenate(xor_gather(upstream.astype(BF), "fsdp"), axis=0)
    mixer_b, window, upstream_all = lax.optimization_barrier((normed_b, window, upstream_all))
    mixed = matmul(mixer_b, mamba_proj)
    attended, log_total = attend(query, window, pos_column)
    attend_branch = matmul(attended, attend_out)
    raw = mixed[:, DIN + XBC :]
    last_rows = mixed[length - 8 :, DIN : DIN + XBC].astype(BF)
    edge = shift(last_rows, "ctx", 1)
    bias_row, rate_row, gated_row = (bias_f[None], rate_f[None], gated_f[None])
    skip_row = jnp.repeat(skip_f, MHEAD)[None]
    step, cum, cum_rows = mamba_prep(raw, bias_row, rate_row)
    decay = jnp.exp(cum[length - 1])
    act = mamba_conv(mixed, edge, taps_f)
    y_local, local_state = mamba_scan(act, step, cum, cum_rows, skip_row)
    incoming = carried(local_state, decay, "ctx", 1)
    scan_out, mamba_normed_b, inverse_three = mamba_finish(
        y_local, mixed, act, cum, incoming, gated_row
    )
    middle = tokens + attend_branch + matmul(mamba_normed_b, mamba_back_w)
    feed_normed, inverse_two = rms_forward(middle, feed_f)
    feed_b = feed_normed.astype(BF)
    rows_all = jnp.concatenate(xor_gather(feed_b, "fsdp"), axis=0)

    gate, up, activated = feed_forward(rows_all, gate_weight, up_weight)
    act_grad = matmul(upstream_all, down_weight.T)
    sigma = jax.nn.sigmoid(gate)
    gate_part = (act_grad * up * sigma * (1.0 + gate * (1.0 - sigma))).astype(BF)
    up_part = (act_grad * gate * sigma).astype(BF)
    feed_back = matmul(gate_part, gate_weight.T) + matmul(up_part, up_weight.T)
    feed_grads = (
        matmul(rows_all.T, gate_part).astype(BF),
        matmul(rows_all.T, up_part).astype(BF),
        matmul(activated.T, upstream_all).astype(BF),
    )
    feed_totals = lax.psum(feed_grads, "ctx")
    feed_grad = xor_scatter(jnp.split(feed_back, group, axis=0), "fsdp")
    feed_grad, feed_grads = lax.optimization_barrier((feed_grad, feed_grads))
    feed_out = xor_scatter(jnp.split(matmul(activated, down_weight), group, axis=0), "fsdp")
    output = middle + feed_out

    back_two, feed_gain_grad = rms_backward(middle, inverse_two, feed_f, feed_grad)
    middle_grad = upstream + back_two
    middle_b = middle_grad.astype(BF)
    out_columns = jnp.concatenate(
        [
            part
            for pair in zip(column_blocks(attended, "fsdp"), column_blocks(mamba_normed_b, "fsdp"))
            for part in pair
        ],
        axis=1,
    )
    out_grads = xor_scatter(jnp.split(matmul(out_columns.T, middle_b), group, axis=0), "fsdp")
    out_totals = all_sum(out_grads, "ctx")

    normed_mamba_grad = matmul(middle_b, mamba_back_w.T)
    dy, gate_z_grad, grad_incoming, gated_gain_grad = mamba_gate_back(
        normed_mamba_grad, scan_out, mixed, act, cum, gated_row, inverse_three
    )
    normed_columns = jnp.concatenate(column_blocks(normed_b, "fsdp"), axis=1)

    def input_weight_grad(grad):
        return jnp.split(matmul(normed_columns.T, grad), group, axis=0)

    gate_columns = all_sum(xor_scatter(input_weight_grad(gate_z_grad), "fsdp"), "ctx", 1)
    state_grad = carried(grad_incoming, decay, "ctx", -1)
    dx, dbc, dstep, dcum, dskip = mamba_scan_back(
        act, step, cum, cum_rows, skip_row, scan_out, dy, incoming
    )
    conv_grad, head_rows, taps_grad, dstep, dcum = mamba_conv_back(
        mixed, edge, taps_f, act, dx, dbc, state_grad, incoming, step, cum, dstep, dcum
    )
    raw_grad, bias_grad, rate_grad = mamba_step_back(raw, bias_row, rate_row, step, dstep, dcum)
    skip_grad = jnp.sum(dskip.reshape(MHEADS, MHEAD), axis=1)
    returned = shift(head_rows, "ctx", -1)
    conv_grad = jnp.concatenate(
        [conv_grad[: length - 8], conv_grad[length - 8 :] + returned], axis=0
    )
    rest_grad = jnp.concatenate([conv_grad.astype(BF), raw_grad.astype(BF)], axis=1)
    rest_columns = all_sum(xor_scatter(input_weight_grad(rest_grad), "fsdp"), "ctx")
    mixed_grad = jnp.concatenate([gate_z_grad, rest_grad], axis=1)
    normed_grad = matmul(mixed_grad, mamba_proj.T)

    attended_grad = matmul(middle_b, attend_out.T).astype(BF)
    query_grad, window_back = attend_back(
        query, window, pos_column, attended, attended_grad, log_total, cosine, sine
    )
    pieces = jnp.split(window_back, reach + 1, axis=0)
    kv_grad = pl.pallas_call(
        functools.partial(join_kernel, reach),
        out_shape=jax.ShapeDtypeStruct((length, 2 * KVDIM), BF),
        name="join",
    )(
        pieces[reach],
        *[shift(pieces[reach - k], "ctx", -k) for k in range(1, reach + 1)],
        cosine,
        sine,
    )
    projected_grad = jnp.concatenate([query_grad, kv_grad], axis=1)
    normed_grad = normed_grad + matmul(projected_grad, attend_in.T)
    back_one, mixer_gain_grad = rms_backward(tokens, inverse_one, mixer_f, normed_grad)
    input_grad = middle_grad + back_one

    small_grads = jnp.concatenate(
        [
            mixer_gain_grad.reshape(group, -1),
            feed_gain_grad.reshape(group, -1),
            gated_gain_grad.reshape(group, -1),
            taps_grad.reshape(CONV, group, -1).transpose(1, 0, 2).reshape(group, -1),
            bias_grad.reshape(group, -1),
            rate_grad.reshape(group, -1),
            skip_grad.reshape(group, -1),
        ],
        axis=1,
    )
    mine = lax.axis_index("fsdp")
    width = projected_grad.shape[1]
    spare = -(-small_grads.shape[1] // (ctx_count * width)) * ctx_count
    small_grads = jnp.pad(
        small_grads, ((0, 0), (0, spare * width - small_grads.shape[1]))
    ).reshape(group, spare, width)
    last = all_sum(
        xor_scatter(
            [
                jnp.concatenate(
                    [part, lax.dynamic_index_in_dim(small_grads, mine ^ d, 0, False)], axis=0
                )
                for d, part in enumerate(input_weight_grad(projected_grad))
            ],
            "fsdp",
        ),
        "ctx",
        1,
    )
    attend_in_total, small_total = (last[: attention_in.shape[0]], last[attention_in.shape[0] :])
    small_total = small_total.reshape(-1)
    total_mixer, total_feed, total_gated, total_taps, total_bias, total_rate, total_skip = (
        small_total[bounds[k] : bounds[k + 1]].astype(F32) for k in range(len(sizes))
    )
    return (
        output[None],
        input_grad[None],
        total_mixer,
        attend_in_total.astype(F32),
        out_totals[:attend_rows].astype(F32),
        jnp.concatenate([gate_columns, rest_columns], axis=1).astype(F32),
        total_taps.reshape(CONV, -1),
        total_bias,
        total_rate,
        total_skip,
        total_gated,
        out_totals[attend_rows:].astype(F32),
        total_feed,
        *(part.astype(F32) for part in feed_totals),
    )


def solution(mesh):
    return jax.shard_map(
        body,
        mesh=mesh,
        in_specs=(
            P("fsdp", "ctx", None),
            P("fsdp", "ctx"),
            P("fsdp"),
            P("fsdp", None),
            P("fsdp", None),
            P("fsdp", None),
            P(None, "fsdp"),
            P("fsdp"),
            P("fsdp"),
            P("fsdp"),
            P("fsdp"),
            P("fsdp", None),
            P("fsdp"),
            P(None, "fsdp"),
            P(None, "fsdp"),
            P("fsdp", None),
            P("fsdp", "ctx", None),
        ),
        out_specs=(
            P("fsdp", "ctx", None),
            P("fsdp", "ctx", None),
            P("fsdp"),
            P("fsdp", None),
            P("fsdp", None),
            P("fsdp", None),
            P(None, "fsdp"),
            P("fsdp"),
            P("fsdp"),
            P("fsdp"),
            P("fsdp"),
            P("fsdp", None),
            P("fsdp"),
            P(None, "fsdp"),
            P(None, "fsdp"),
            P("fsdp", None),
        ),
        check_vma=False,
    )
```
